512 devices in a mesh: rep: 64 (over z, y), row: 8 (over x, core).
Axes of the slice: x: 4, y: 4, z: 16, core: 2. Of those that a mesh axis runs over, the one named last changes fastest.
Arguments:
- momentum: float32 [64, 8192, 128], P('rep', 'row'), may hold values from -6 to 6
- inputs: bfloat16 [64, 1024, 8192], P('rep', None, 'row'), may hold values from -6 to 6
- out_grads: bfloat16 [64, 1024, 128], P('rep', 'row'), may hold values from -0.19921875 to 0.19921875
- chosen: int32 [64, 64, 1, 8], P('rep', 'row'), may hold values from 0 to 128, as said below
Outputs:
- new_momentum: float32 [64, 8192, 128], P('rep', 'row')
- update: float32 [8192, 128], P('row')
The draws below stay inside these ranges and needn't reach their ends.
Inputs may be any that keep to these rules, and one draw needn't show every extreme that they name: `chosen`: for each replica and block, the first c entries, with 1 <= c <= 8, are distinct coefficient rows below 128, and the remaining entries equal 128; on every device the first block has 8 entries.
All inputs are finite; a program needn't handle non-finite values.
Results may differ from the reference program's by a relative error of at most 0.0003.
Values may be sent and summed in bfloat16 or wider, within the bound.
No kernel may reach another device: no remote copies, remote signals or barrier semaphores. Data moves between devices by JAX's collectives and lax.ppermute only.
A program may use at most 64 MiB of HBM per device.

```python
import jax
import jax.numpy as jnp
from jax import lax

D = 8192
CH = 128
CBLK = 1
TOK = 1024
K = 8
COLS = 128
RBLK = 8
REPS = 64
N_REP = 64


def draw_chosen(key, part):
    block_rows = D // CH
    leading = N_REP * block_rows * CBLK
    order_keys = jax.random.split(jax.random.fold_in(key, 11), leading)
    orders = jax.vmap(lambda one_key: jax.random.permutation(one_key, CH)[:K])(order_keys)
    counts = jax.random.randint(jax.random.fold_in(key, 12), (leading,), 1, K + 1)
    flat_index = jnp.arange(leading)
    column_block = flat_index % CBLK
    row_block = flat_index // CBLK % block_rows
    forced = (column_block == 0) & (row_block % RBLK == 0)
    counts = jnp.where(forced, K, counts)
    slot_index = jnp.arange(K)[None, :]
    result = jnp.where(slot_index < counts[:, None], orders, CH)
    return result.reshape(N_REP, block_rows, CBLK, K).astype(jnp.int32)


def block_levels(own_key, shape, pieces, smallest, top_value):
    factor_of, own = 1.0, jax.random.fold_in(own_key, 6)
    for dim, shards_of in pieces:
        steps = jnp.exp(jax.random.uniform(jax.random.fold_in(own, dim), (shards_of,), jnp.float32, smallest / len(pieces), top_value / len(pieces)))
        factor_of = factor_of * jnp.repeat(steps, shape[dim] // shards_of).reshape([-1 if axis == dim else 1 for axis in range(len(shape))])
    return factor_of


def normal_values(rng, shape, width, most, shards=(), kind=jnp.bfloat16):
    array = jax.random.normal(rng, shape, jnp.float32) * width
    if len(shards) > 0:
        array = block_levels(rng, shape, shards, -0.22, 0.18) * array
    return jnp.clip(array, min=-most, max=most).astype(kind)


def setup_inputs(seed: int = 0) -> dict:
    keys = jax.random.split(jax.random.key(seed), 5)
    momentum = normal_values(keys[0], (REPS, D, COLS), 1.0, 6.0, ((0, 64), (1, 8)), jnp.float32)
    inputs = normal_values(keys[1], (REPS, TOK, D), 1.0, 6.0, ((0, 64), (2, 8)))
    out_grads = normal_values(keys[2], (REPS, TOK, COLS), 0.03125, 0.19921875, ((0, 64), (1, 8)))
    chosen = draw_chosen(jax.random.fold_in(keys[4], 71), 0)
    return dict(momentum=momentum, inputs=inputs, out_grads=out_grads, chosen=chosen)


PRECISE = lax.Precision.HIGHEST
MOMENTUM_DECAY = 0.999

def basis_table(order):
    frequency = jnp.arange(order, dtype=jnp.float32)[:, None]
    sample = jnp.arange(order, dtype=jnp.float32)[None, :]
    norm_scale = jnp.where(frequency == 0.0, jnp.sqrt(1.0 / order), jnp.sqrt(2.0 / order))
    return norm_scale * jnp.cos(jnp.pi * (2.0 * sample + 1.0) * frequency / (2.0 * order))

def to_blocks(matrix):
    row_total, col_total = matrix.shape
    return matrix.reshape(row_total // CH, CH, col_total // CH, CH).transpose(0, 2, 1, 3)

def from_blocks(blocks):
    row_blocks, col_blocks = (blocks.shape[0], blocks.shape[1])
    return blocks.transpose(0, 2, 1, 3).reshape(row_blocks * CH, col_blocks * CH)

def forward(blocks, basis):
    left = jnp.einsum('kn,abnm->abkm', basis, blocks, precision=PRECISE)
    return jnp.einsum('abkm,jm->abkj', left, basis, precision=PRECISE)

def inverse(coeffs, basis):
    left = jnp.einsum('kn,abkj->abnj', basis, coeffs, precision=PRECISE)
    return jnp.einsum('abnj,jm->abnm', left, basis, precision=PRECISE)

def reference(momentum, inputs, out_grads, chosen):
    basis = basis_table(CH)

    def replica(summed, entry):
        moment_old, activations, grads_out, chosen_rows = entry
        weight_grad = jnp.dot(activations.T, grads_out, preferred_element_type=jnp.float32)
        moment = MOMENTUM_DECAY * moment_old + weight_grad
        coeffs = forward(to_blocks(moment), basis)
        one_hot = (chosen_rows[..., None] == jnp.arange(CH, dtype=jnp.int32)).astype(jnp.float32)
        selected = jnp.einsum('abqk,abkj->abqj', one_hot, coeffs, precision=PRECISE)
        placed = jnp.einsum('abqk,abqj->abkj', one_hot, selected, precision=PRECISE)
        moment_new = moment - from_blocks(inverse(placed, basis))
        return (summed + placed, moment_new)
    start_sum = jnp.zeros((D // CH, CBLK, CH, CH), jnp.float32)
    summed, new_momentum = lax.scan(replica, start_sum, (momentum, inputs, out_grads, chosen))
    update = from_blocks(inverse(summed, basis))
    return (new_momentum, update)
```

```python
import jax
import jax.numpy as jnp
import numpy as np
from jax import lax
from jax.experimental import pallas as pl
from jax.experimental.pallas import tpu as pltpu
from jax.sharding import PartitionSpec as P

CH = 128
K = 8
BLOCKS = 8
GROUPS = 8
WIDTH = CH // GROUPS
REPS = 64
NZ, NY = 16, 4
MOMENTUM_DECAY = 0.999
HIGHEST = lax.Precision.HIGHEST

Z_GROUPS = [[z * NY + y for z in range(NZ)] for y in range(NY)]
Y_GROUPS = [[z * NY + y for y in range(NY)] for z in range(NZ)]


def basis_rows():
    frequency = np.arange(CH, dtype=np.float64)[:, None]
    sample = np.arange(CH, dtype=np.float64)[None, :]
    scale = np.where(frequency == 0.0, np.sqrt(1.0 / CH), np.sqrt(2.0 / CH))
    basis = scale * np.cos(np.pi * (2.0 * sample + 1.0) * frequency / (2.0 * CH))
    return np.concatenate([basis, np.zeros((8, CH))]).astype(np.float32)


def dot(a, b, dims):
    return lax.dot_general(a, b, (dims, ((), ())), precision=HIGHEST, preferred_element_type=jnp.float32)


def project(chosen_s, chosen_v, basis, momentum, inputs, grads, new_momentum, message, picked, partial):
    for i in range(BLOCKS * K):
        row = chosen_s[i // K, i % K]
        picked[i : i + 1, :] = basis[pl.ds(row, 1), :]
    grad = lax.dot_general(
        inputs[...], grads[...], (((0,), (0,)), ((), ())), preferred_element_type=jnp.float32
    )
    for b in range(BLOCKS):
        rows = slice(b * CH, (b + 1) * CH)
        moment = MOMENTUM_DECAY * momentum[rows, :] + grad[rows, :]
        own = picked[b * K : (b + 1) * K, :]
        left = dot(own, moment, ((1,), (0,)))
        partial[b * K : (b + 1) * K, :] = left
        new_momentum[rows, :] = moment - dot(own, left, ((0,), (0,)))
    slot = lax.broadcasted_iota(jnp.int32, (BLOCKS, CH), 1) // WIDTH
    places = jnp.zeros((BLOCKS, CH), jnp.float32)
    per_slot = []
    for q in range(K):
        places = jnp.where(slot == q, chosen_v[:, q : q + 1].astype(jnp.float32), places)
        per_slot.append(partial[pl.ds(q, BLOCKS, stride=K), :])
    for g in range(GROUPS):
        row = jnp.zeros((BLOCKS, CH), jnp.float32)
        for q in range(K):
            turn = ((q - g) * WIDTH) % CH
            moved = per_slot[q] if turn == 0 else pltpu.roll(per_slot[q], turn, 1)
            row = jnp.where(slot == q, moved, row)
        message[g * BLOCKS : (g + 1) * BLOCKS, 0, :] = row
        message[g * BLOCKS : (g + 1) * BLOCKS, 1, :] = places


def combine(basis, received, piece):
    values = received[:, 0, :].T
    places = received[:, 1, :].astype(jnp.int32)
    rows = lax.broadcasted_iota(jnp.int32, (REPS, CH), 1)
    total = jnp.zeros((WIDTH, CH), jnp.float32)
    for q in range(K):
        hot = (places[:, q * WIDTH : q * WIDTH + 1] == rows).astype(jnp.float32)
        total = total + dot(values[q * WIDTH : (q + 1) * WIDTH, :], hot, ((1,), (0,)))
    done = dot(total, basis[:CH, :], ((1,), (0,)))
    for z in range(NZ):
        piece[z, :, :] = done


def place(gathered, update):
    for b in range(BLOCKS):
        parts = [gathered[b % NY, 2 * g + b // NY, :, :] for g in range(GROUPS)]
        update[b * CH : (b + 1) * CH, :] = jnp.concatenate(parts, axis=0).T


def in_vmem(n):
    return [pl.BlockSpec(memory_space=pltpu.VMEM)] * n


def body(momentum, inputs, out_grads, chosen):
    table = jnp.asarray(basis_rows())
    picks = chosen.reshape(BLOCKS, K)
    grads = lax.all_to_all(
        jnp.broadcast_to(out_grads, (8,) + out_grads.shape[1:]), "row", 0, 0, tiled=True
    )
    new_momentum, message = pl.pallas_call(
        project,
        name="project",
        out_shape=(
            jax.ShapeDtypeStruct((BLOCKS * CH, CH), jnp.float32),
            jax.ShapeDtypeStruct((REPS, 2, CH), jnp.float32),
        ),
        in_specs=[pl.BlockSpec(memory_space=pltpu.SMEM)] + in_vmem(5),
        out_specs=tuple(in_vmem(2)),
        scratch_shapes=[
            pltpu.VMEM((BLOCKS * K, CH), jnp.float32),
            pltpu.VMEM((BLOCKS * K, CH), jnp.float32),
        ],
    )(picks, picks, table, momentum[0], inputs[0], grads.reshape(-1, CH))
    received = lax.all_to_all(message, "rep", 0, 0, tiled=True)
    piece = pl.pallas_call(
        combine,
        name="combine",
        out_shape=jax.ShapeDtypeStruct((NZ, WIDTH, CH), jnp.float32),
        in_specs=in_vmem(2),
        out_specs=in_vmem(1)[0],
    )(table, received)
    along_z = lax.all_to_all(piece, "rep", 0, 0, axis_index_groups=Z_GROUPS, tiled=True)
    along_y = lax.all_to_all(
        jnp.broadcast_to(along_z, (NY,) + along_z.shape), "rep", 0, 0, axis_index_groups=Y_GROUPS, tiled=True
    )
    update = pl.pallas_call(
        place,
        name="place",
        out_shape=jax.ShapeDtypeStruct((BLOCKS * CH, CH), jnp.float32),
        in_specs=in_vmem(1),
        out_specs=in_vmem(1)[0],
    )(along_y)
    return new_momentum[None], update


def solution(mesh):
    in_specs = (
        P("rep", "row", None),
        P("rep", None, "row"),
        P("rep", "row", None),
        P("rep", "row", None, None),
    )
    out_specs = (P("rep", "row", None), P("row", None))
    return jax.shard_map(body, mesh=mesh, in_specs=in_specs, out_specs=out_specs, check_vma=False)
```

```python
import jax
import jax.numpy as jnp
import numpy as np
from jax import lax
from jax.experimental import pallas as pl
from jax.experimental.pallas import tpu as pltpu
from jax.sharding import PartitionSpec as P

CH = 128
K = 8
BLOCKS = 8
PICKS = BLOCKS * K
ROWS = 8
TOK = 1024
NZ, NY = 16, 4
MOMENTUM_DECAY = 0.999
BITS = 15
TOP = 32767.0
HIGHEST = lax.Precision.HIGHEST
F32, BF16, I32, I16 = jnp.float32, jnp.bfloat16, jnp.int32, jnp.int16

Z_GROUPS = [[z * NY + y for z in range(NZ)] for y in range(NY)]
Y_GROUPS = [[z * NY + y for y in range(NY)] for z in range(NZ)]


def basis_rows():
    frequency = np.arange(CH, dtype=np.float64)[:, None]
    sample = np.arange(CH, dtype=np.float64)[None, :]
    scale = np.where(frequency == 0.0, np.sqrt(1.0 / CH), np.sqrt(2.0 / CH))
    basis = scale * np.cos(np.pi * (2.0 * sample + 1.0) * frequency / (2.0 * CH))
    return np.concatenate([basis, np.zeros((8, CH))]).astype(np.float32)


def dot(a, b, dims, precision=None):
    return lax.dot_general(a, b, (dims, ((), ())), precision=precision, preferred_element_type=F32)


def halves(a):
    high = a.astype(BF16)
    return high, (a - high.astype(F32)).astype(BF16)


def block(b):
    return slice(b * CH, (b + 1) * CH)


def picks(b):
    return slice(b * K, (b + 1) * K)


def exponent(values, axis):
    most = jnp.max(jnp.abs(values), axis=axis, keepdims=True)
    return jnp.ceil(jnp.log2(jnp.maximum(most, 1e-30)) + 0.01)


def encode(values, power):
    scaled = jnp.round(values * jnp.exp2(BITS - power))
    return jnp.clip(scaled, -TOP, TOP).astype(I32)


def prepare(chosen, basis, momentum, inputs, picked, base, weights, places):
    slot = lax.broadcasted_iota(I32, (K, CH), 0)
    lane = lax.broadcasted_iota(I32, (K, CH), 1)
    numbers = jnp.zeros((K, CH), I32)
    for i in range(PICKS):
        b, q = i // K, i % K
        row = chosen[b, q]
        picked[i : i + 1, :] = basis[pl.ds(row, 1), :]
        numbers = jnp.where((slot == q) & (lane == b), row, numbers)
    places[...] = numbers
    for b in range(BLOCKS):
        own = picked[picks(b), :]
        base[picks(b), :] = dot(own, MOMENTUM_DECAY * momentum[block(b), :], ((1,), (0,)), HIGHEST)
        both = jnp.concatenate(halves(own), axis=0)
        product = dot(both, inputs[:, block(b)], ((1,), (1,)))
        high, low = halves(product[:K] + product[K:])
        weights[picks(b), :] = high
        weights[PICKS + b * K : PICKS + (b + 1) * K, :] = low


def pack(base, weights, places, grads, message, left):
    product = dot(weights[...], grads[...], ((1,), (0,)))
    own = base[...] + product[:PICKS] + product[PICKS:]
    left[...] = own
    power = exponent(own, 1)
    codes = encode(own, power).astype(I16)
    lane = lax.broadcasted_iota(I32, (K, CH), 1)
    notes = places[...]
    for b in range(BLOCKS):
        notes = jnp.where(lane == BLOCKS + b, power[picks(b), :].astype(I32), notes)
    notes = notes.astype(I16)
    for z in range(NZ):
        message[z, :PICKS, :] = codes
        message[z, PICKS:, :] = notes


def subtract(picked, left, momentum, inputs, grads, new_momentum, done):
    grad = dot(inputs[...], grads[...], ((0,), (0,)))
    for b in range(BLOCKS):
        sent = dot(picked[picks(b), :], left[picks(b), :], ((0,), (0,)), HIGHEST)
        new_momentum[block(b), :] = MOMENTUM_DECAY * momentum[block(b), :] + grad[block(b), :] - sent
    done[...] = picked[:8, :]


def combine(basis, received, after, message):
    del after
    notes = received[:, PICKS:, :].astype(I32).reshape(NZ * K, CH)
    scales = jnp.exp2(notes.astype(F32) - BITS)
    rows = lax.broadcasted_iota(I32, (NZ * K, CH), 1)
    powers = []
    for b in range(BLOCKS):
        codes = received[:, picks(b), :].astype(I32).reshape(NZ * K, CH)
        high = lax.shift_right_arithmetic(codes, 8)
        low = codes - high * 256
        terms = jnp.concatenate([high.astype(F32).astype(BF16), low.astype(F32).astype(BF16)], axis=1)
        hot = jnp.where(notes[:, b : b + 1] == rows, scales[:, BLOCKS + b : BLOCKS + b + 1], 0.0).astype(BF16)
        sums = dot(hot, terms, ((0,), (0,)))
        own = dot(basis[:CH, :], 256.0 * sums[:, :CH] + sums[:, CH:], ((0,), (0,)), HIGHEST)
        power = exponent(own, 0)
        powers.append(power)
        coded = encode(own, power).astype(I16)
        for y in range(NY):
            message[y, block(b), :] = coded
    powers = jnp.concatenate(powers, axis=0).astype(I32).astype(I16)
    for y in range(NY):
        message[y, BLOCKS * CH :, :] = powers


def finish(received, update):
    for b in range(BLOCKS):
        total = jnp.zeros((CH, CH), F32)
        for y in range(NY):
            power = received[y, BLOCKS * CH :, :].astype(I32)[b : b + 1, :].astype(F32)
            total = total + received[y, block(b), :].astype(I32).astype(F32) * jnp.exp2(power - BITS)
        update[block(b), :] = total


def call(kernel, out, operands, spaces=None, flops=0, limit=4, scratch=()):
    spaces = spaces or [pltpu.VMEM] * len(operands)
    moved = sum(a.size * a.dtype.itemsize for a in operands) + sum(o.size * o.dtype.itemsize for o in out)
    return pl.pallas_call(
        kernel,
        name=kernel.__name__,
        out_shape=tuple(out),
        in_specs=[pl.BlockSpec(memory_space=s) for s in spaces],
        out_specs=tuple(pl.BlockSpec(memory_space=pltpu.VMEM) for _ in out),
        scratch_shapes=list(scratch),
        compiler_params=pltpu.CompilerParams(vmem_limit_bytes=int(limit * 2**20)),
        cost_estimate=pl.CostEstimate(flops=flops, bytes_accessed=moved, transcendentals=0),
    )(*operands)


def array(shape, dtype=F32):
    return jax.ShapeDtypeStruct(shape, dtype)


def body(momentum, inputs, out_grads, chosen):
    momentum, inputs = momentum[0], inputs[0]
    table = jnp.asarray(basis_rows())
    copies = jnp.broadcast_to(out_grads, (ROWS,) + out_grads.shape[1:])
    grads = lax.all_to_all(copies, "row", 0, 0, tiled=True).reshape(TOK, CH)
    picked, base, weights, places = call(
        prepare,
        [array((PICKS, CH)), array((PICKS, CH)), array((2 * PICKS, TOK), BF16), array((K, CH), I32)],
        [chosen.reshape(BLOCKS, K), table, momentum, inputs],
        spaces=[pltpu.SMEM, pltpu.VMEM, pltpu.VMEM, pltpu.VMEM],
        flops=2 * 2 * PICKS * CH * TOK,
    )
    message, left = call(
        pack,
        [array((NZ, PICKS + K, CH), I16), array((PICKS, CH))],
        [base, weights, places, grads],
        flops=2 * 2 * PICKS * CH * TOK,
    )
    along_z = lax.all_to_all(message, "rep", 0, 0, axis_index_groups=Z_GROUPS, tiled=True)
    new_momentum, after = call(
        subtract,
        [array((BLOCKS * CH, CH)), array((8, CH))],
        [picked, left, momentum, inputs, grads],
        flops=2 * BLOCKS * CH * CH * TOK,
    )
    (message,) = call(
        combine,
        [array((NY, BLOCKS * CH + BLOCKS, CH), I16)],
        [table, along_z, after],
        limit=8,
    )
    along_y = lax.all_to_all(message, "rep", 0, 0, axis_index_groups=Y_GROUPS, tiled=True)
    (update,) = call(finish, [array((BLOCKS * CH, CH))], [along_y])
    return new_momentum[None], update


def solution(mesh):
    in_specs = (
        P("rep", "row", None),
        P("rep", None, "row"),
        P("rep", "row", None),
        P("rep", "row", None, None),
    )
    out_specs = (P("rep", "row", None), P("row", None))
    return jax.shard_map(body, mesh=mesh, in_specs=in_specs, out_specs=out_specs, check_vma=False)
```

```python
import jax
import jax.numpy as jnp
import numpy as np
from jax import lax
from jax.experimental import pallas as pl
from jax.experimental.pallas import tpu as pltpu
from jax.sharding import PartitionSpec as P

CH = 128
K = 8
BLOCKS = 8
PICKS = BLOCKS * K
ROWS = 8
TOK = 1024
NZ, NY = 16, 4
MOMENTUM_DECAY = 0.999
BITS = 15
TOP = 32767.0
HIGHEST = lax.Precision.HIGHEST
F32, BF16, I32, I16 = jnp.float32, jnp.bfloat16, jnp.int32, jnp.int16

Z_GROUPS = [[z * NY + y for z in range(NZ)] for y in range(NY)]
Y_GROUPS = [[z * NY + y for y in range(NY)] for z in range(NZ)]


def basis_rows():
    frequency = np.arange(CH, dtype=np.float64)[:, None]
    sample = np.arange(CH, dtype=np.float64)[None, :]
    scale = np.where(frequency == 0.0, np.sqrt(1.0 / CH), np.sqrt(2.0 / CH))
    basis = scale * np.cos(np.pi * (2.0 * sample + 1.0) * frequency / (2.0 * CH))
    return np.concatenate([basis, np.zeros((8, CH))]).astype(np.float32)


def dot(a, b, dims, precision=None):
    return lax.dot_general(a, b, (dims, ((), ())), precision=precision, preferred_element_type=F32)


def halves(a):
    high = a.astype(BF16)
    return high, (a - high.astype(F32)).astype(BF16)


def block(b):
    return slice(b * CH, (b + 1) * CH)


def picks(b):
    return slice(b * K, (b + 1) * K)


def exponent(values, axis):
    most = jnp.max(jnp.abs(values), axis=axis, keepdims=True)
    return jnp.ceil(jnp.log2(jnp.maximum(most, 1e-30)) + 0.01)


def encode(values, power):
    scaled = jnp.round(values * jnp.exp2(BITS - power))
    return jnp.clip(scaled, -TOP, TOP).astype(I32)


def prepare(chosen, basis, momentum, inputs, picked, base, weights, places):
    slot = lax.broadcasted_iota(I32, (K, CH), 0)
    lane = lax.broadcasted_iota(I32, (K, CH), 1)
    numbers = jnp.zeros((K, CH), I32)
    for i in range(PICKS):
        b, q = i // K, i % K
        row = chosen[b, q]
        picked[i : i + 1, :] = basis[pl.ds(row, 1), :]
        numbers = jnp.where((slot == q) & (lane == b), row, numbers)
    places[...] = numbers
    for b in range(BLOCKS):
        own = picked[picks(b), :]
        base[picks(b), :] = dot(own, MOMENTUM_DECAY * momentum[block(b), :], ((1,), (0,)), HIGHEST)
        both = jnp.concatenate(halves(own), axis=0)
        product = dot(both, inputs[:, block(b)], ((1,), (1,)))
        high, low = halves(product[:K] + product[K:])
        weights[picks(b), :] = high
        weights[PICKS + b * K : PICKS + (b + 1) * K, :] = low


def pack(base, weights, places, grads, message, left):
    product = dot(weights[...], grads[...], ((1,), (0,)))
    own = base[...] + product[:PICKS] + product[PICKS:]
    left[...] = own
    power = exponent(own, 1)
    codes = encode(own, power).astype(I16)
    lane = lax.broadcasted_iota(I32, (K, CH), 1)
    notes = places[...]
    for b in range(BLOCKS):
        notes = jnp.where(lane == BLOCKS + b, power[picks(b), :].astype(I32), notes)
    notes = notes.astype(I16)
    for z in range(NZ):
        message[z, :PICKS, :] = codes
        message[z, PICKS:, :] = notes


def subtract(picked, left, momentum, inputs, grads, new_momentum, done):
    grad = dot(inputs[...], grads[...], ((0,), (0,)))
    for b in range(BLOCKS):
        sent = dot(picked[picks(b), :], left[picks(b), :], ((0,), (0,)), HIGHEST)
        new_momentum[block(b), :] = MOMENTUM_DECAY * momentum[block(b), :] + grad[block(b), :] - sent
    done[...] = picked[:8, :]


def combine(basis, received, after, message):
    del after
    notes = received[:, PICKS:, :].astype(I32).reshape(NZ * K, CH)
    scales = jnp.exp2(notes.astype(F32) - BITS)
    rows = lax.broadcasted_iota(I32, (NZ * K, CH), 1)
    powers = []
    for b in range(BLOCKS):
        codes = received[:, picks(b), :].astype(I32).reshape(NZ * K, CH)
        high = lax.shift_right_arithmetic(codes, 8)
        low = codes - high * 256
        terms = jnp.concatenate([high.astype(F32).astype(BF16), low.astype(F32).astype(BF16)], axis=1)
        hot = jnp.where(notes[:, b : b + 1] == rows, scales[:, BLOCKS + b : BLOCKS + b + 1], 0.0).astype(BF16)
        sums = dot(hot, terms, ((0,), (0,)))
        own = dot(basis[:CH, :], 256.0 * sums[:, :CH] + sums[:, CH:], ((0,), (0,)), HIGHEST)
        power = exponent(own, 0)
        powers.append(power)
        message[block(b), :] = encode(own, power).astype(I16)
    message[BLOCKS * CH :, :] = jnp.concatenate(powers, axis=0).astype(I32).astype(I16)


def finish(received, update):
    for b in range(BLOCKS):
        total = jnp.zeros((CH, CH), F32)
        for y in range(NY):
            power = received[y, BLOCKS * CH :, :].astype(I32)[b : b + 1, :].astype(F32)
            total = total + received[y, block(b), :].astype(I32).astype(F32) * jnp.exp2(power - BITS)
        update[block(b), :] = total


def call(kernel, out, operands, spaces=None, flops=0, limit=4, scratch=()):
    spaces = spaces or [pltpu.VMEM] * len(operands)
    moved = sum(a.size * a.dtype.itemsize for a in operands) + sum(o.size * o.dtype.itemsize for o in out)
    return pl.pallas_call(
        kernel,
        name=kernel.__name__,
        out_shape=tuple(out),
        in_specs=[pl.BlockSpec(memory_space=s) for s in spaces],
        out_specs=tuple(pl.BlockSpec(memory_space=pltpu.VMEM) for _ in out),
        scratch_shapes=list(scratch),
        compiler_params=pltpu.CompilerParams(vmem_limit_bytes=int(limit * 2**20)),
        cost_estimate=pl.CostEstimate(flops=flops, bytes_accessed=moved, transcendentals=0),
    )(*operands)


def array(shape, dtype=F32):
    return jax.ShapeDtypeStruct(shape, dtype)


def body(momentum, inputs, out_grads, chosen):
    momentum, inputs = momentum[0], inputs[0]
    table = jnp.asarray(basis_rows())
    copies = jnp.broadcast_to(out_grads, (ROWS,) + out_grads.shape[1:])
    grads = lax.all_to_all(copies, "row", 0, 0, tiled=True).reshape(TOK, CH)
    picked, base, weights, places = call(
        prepare,
        [array((PICKS, CH)), array((PICKS, CH)), array((2 * PICKS, TOK), BF16), array((K, CH), I32)],
        [chosen.reshape(BLOCKS, K), table, momentum, inputs],
        spaces=[pltpu.SMEM, pltpu.VMEM, pltpu.VMEM, pltpu.VMEM],
        flops=2 * 2 * PICKS * CH * TOK,
    )
    message, left = call(
        pack,
        [array((NZ, PICKS + K, CH), I16), array((PICKS, CH))],
        [base, weights, places, grads],
        flops=2 * 2 * PICKS * CH * TOK,
    )
    along_z = lax.all_to_all(message, "rep", 0, 0, axis_index_groups=Z_GROUPS, tiled=True)
    new_momentum, after = call(
        subtract,
        [array((BLOCKS * CH, CH)), array((8, CH))],
        [picked, left, momentum, inputs, grads],
        flops=2 * BLOCKS * CH * CH * TOK,
    )
    (message,) = call(
        combine,
        [array((BLOCKS * CH + BLOCKS, CH), I16)],
        [table, along_z, after],
        limit=8,
    )
    along_y = lax.all_gather(message, "rep", axis_index_groups=Y_GROUPS)
    (update,) = call(finish, [array((BLOCKS * CH, CH))], [along_y])
    return new_momentum[None], update


def solution(mesh):
    in_specs = (
        P("rep", "row", None),
        P("rep", None, "row"),
        P("rep", "row", None),
        P("rep", "row", None, None),
    )
    out_specs = (P("rep", "row", None), P("row", None))
    return jax.shard_map(body, mesh=mesh, in_specs=in_specs, out_specs=out_specs, check_vma=False)
```

```python
import jax
import jax.numpy as jnp
import numpy as np
from jax import lax
from jax.experimental import pallas as pl
from jax.experimental.pallas import tpu as pltpu
from jax.sharding import PartitionSpec as P

CH = 128
K = 8
BLOCKS = 8
PICKS = BLOCKS * K
ROWS = 8
PAIR = 2
TOK = 1024
NZ, NY = 16, 4
MOMENTUM_DECAY = 0.999
AHEAD = 10**10
BITS = 15
TOP = 32767.0
HIGHEST = lax.Precision.HIGHEST
F32, BF16, I32, I16 = jnp.float32, jnp.bfloat16, jnp.int32, jnp.int16

Z_GROUPS = [[z * NY + y for z in range(NZ)] for y in range(NY)]
Y_GROUPS = [[z * NY + y for y in range(NY)] for z in range(NZ)]


def basis_rows():
    frequency = np.arange(CH, dtype=np.float64)[:, None]
    sample = np.arange(CH, dtype=np.float64)[None, :]
    scale = np.where(frequency == 0.0, np.sqrt(1.0 / CH), np.sqrt(2.0 / CH))
    basis = scale * np.cos(np.pi * (2.0 * sample + 1.0) * frequency / (2.0 * CH))
    return np.concatenate([basis, np.zeros((8, CH))]).astype(np.float32)


def dot(a, b, dims, precision=None):
    return lax.dot_general(a, b, (dims, ((), ())), precision=precision, preferred_element_type=F32)


def halves(a):
    high = a.astype(BF16)
    return high, (a - high.astype(F32)).astype(BF16)


def block(b):
    return slice(b * CH, (b + 1) * CH)


def picks(b):
    return slice(b * K, (b + 1) * K)


def exponent(values, axis):
    most = jnp.max(jnp.abs(values), axis=axis, keepdims=True)
    return jnp.ceil(jnp.log2(jnp.maximum(most, 1e-30)) + 0.01)


def encode(values, power):
    scaled = jnp.round(values * jnp.exp2(BITS - power))
    return jnp.clip(scaled, -TOP, TOP).astype(I32)


def spread(out_grads, copies):
    for r in range(ROWS):
        copies[r, :, :] = out_grads[...]


def project(chosen, basis, momentum, inputs, grads, message, picked, left):
    slot = lax.broadcasted_iota(I32, (K, CH), 0)
    lane = lax.broadcasted_iota(I32, (K, CH), 1)
    notes = jnp.zeros((K, CH), I32)
    for i in range(PICKS):
        b, q = i // K, i % K
        row = chosen[b, q]
        picked[i : i + 1, :] = basis[pl.ds(row, 1), :]
        notes = jnp.where((slot == q) & (lane == b), row, notes)
    highs, lows, bases = [], [], []
    for b in range(BLOCKS):
        terms = halves(picked[picks(b), :])
        both = jnp.concatenate(terms, axis=0)
        product = dot(both, inputs[:, block(b)], ((1,), (1,)))
        high, low = halves(product[:K] + product[K:])
        highs.append(high)
        lows.append(low)
        high, low = halves(MOMENTUM_DECAY * momentum[block(b), :])
        product = dot(both, high, ((1,), (0,)))
        bases.append(product[:K] + product[K:] + dot(terms[0], low, ((1,), (0,))))
    product = dot(jnp.concatenate(highs + lows, axis=0), grads[...], ((1,), (0,)))
    own = jnp.concatenate(bases, axis=0) + product[:PICKS] + product[PICKS:]
    left[...] = own
    power = exponent(own, 1)
    codes = encode(own, power).astype(I16)
    for b in range(BLOCKS):
        notes = jnp.where(lane == BLOCKS + b, power[picks(b), :].astype(I32), notes)
    notes = notes.astype(I16)
    for z in range(NZ):
        message[z, :PICKS, :] = codes
        message[z, PICKS:, :] = notes


def subtract(picked, left, momentum, inputs, grads, new_momentum, done):
    grad = dot(inputs[...], grads[...], ((0,), (0,)))
    for b in range(BLOCKS):
        sent = dot(picked[picks(b), :], left[picks(b), :], ((0,), (0,)), HIGHEST)
        new_momentum[block(b), :] = MOMENTUM_DECAY * momentum[block(b), :] + grad[block(b), :] - sent
    done[...] = picked[:8, :]


def combine(basis, received, after, message):
    del after
    notes = received[:, PICKS:, :].astype(I32).astype(F32).reshape(NZ * K, CH).T
    scales = jnp.exp2(notes[BLOCKS : 2 * BLOCKS, :] - BITS)
    rows = lax.broadcasted_iota(I32, (CH, NZ * K), 0).astype(F32)
    high, low = halves(basis[:CH, :].T)
    back = jnp.concatenate([high, low], axis=0)
    powers = []
    for b in range(BLOCKS):
        codes = received[:, picks(b), :].astype(I32).astype(F32).reshape(NZ * K, CH)
        hot = jnp.where(notes[b : b + 1, :] == rows, scales[b : b + 1, :], 0.0).astype(BF16)
        sums = dot(hot, jnp.concatenate(halves(codes), axis=1), ((1,), (0,)))
        own = sums[:, :CH] + sums[:, CH:]
        own_high, own_low = halves(own)
        product = dot(back, own_high, ((1,), (0,)))
        own = product[:CH] + product[CH:] + dot(high, own_low, ((1,), (0,)))
        power = exponent(own, 0)
        powers.append(power)
        message[block(b), :] = encode(own, power).astype(I16)
    message[BLOCKS * CH :, :] = jnp.concatenate(powers, axis=0).astype(I32).astype(I16)


def finish(received, update, total, sems):
    scales = [jnp.exp2(received[y, BLOCKS * CH :, :].astype(I32).astype(F32) - BITS) for y in range(NY)]
    stores = []
    for b in range(BLOCKS):
        parts = [received[y, block(b), :].astype(I32).astype(F32) * scales[y][b : b + 1, :] for y in range(NY)]
        total[block(b), :] = parts[0] + parts[1] + (parts[2] + parts[3])
        if b % PAIR == PAIR - 1:
            done = slice((b + 1 - PAIR) * CH, (b + 1) * CH)
            stores.append(pltpu.make_async_copy(total.at[done, :], update.at[done, :], sems.at[b // PAIR]))
            stores[-1].start()
    for store in stores:
        store.wait()


def call(kernel, out, operands, spaces=None, flops=0, limit=4, scratch=(), result=pltpu.VMEM):
    spaces = spaces or [pltpu.VMEM] * len(operands)
    moved = sum(a.size * a.dtype.itemsize for a in operands) + sum(o.size * o.dtype.itemsize for o in out)
    return pl.pallas_call(
        kernel,
        name=kernel.__name__,
        out_shape=tuple(out),
        in_specs=[pl.BlockSpec(memory_space=s) for s in spaces],
        out_specs=tuple(pl.BlockSpec(memory_space=result) for _ in out),
        scratch_shapes=list(scratch),
        compiler_params=pltpu.CompilerParams(vmem_limit_bytes=int(limit * 2**20)),
        cost_estimate=pl.CostEstimate(flops=flops, bytes_accessed=moved, transcendentals=0),
    )(*operands)


def array(shape, dtype=F32):
    return jax.ShapeDtypeStruct(shape, dtype)


def body(momentum, inputs, out_grads, chosen):
    momentum, inputs = momentum[0], inputs[0]
    table = jnp.asarray(basis_rows())
    (copies,) = call(spread, [array((ROWS,) + out_grads.shape[1:], BF16)], [out_grads[0]], flops=AHEAD)
    grads = lax.all_to_all(copies, "row", 0, 0, tiled=True).reshape(TOK, CH)
    message, picked, left = call(
        project,
        [array((NZ, PICKS + K, CH), I16), array((PICKS, CH)), array((PICKS, CH))],
        [chosen.reshape(BLOCKS, K), table, momentum, inputs, grads],
        spaces=[pltpu.SMEM, pltpu.VMEM, pltpu.VMEM, pltpu.VMEM, pltpu.VMEM],
        flops=2 * 2 * 2 * PICKS * CH * TOK,
    )
    along_z = lax.all_to_all(message, "rep", 0, 0, axis_index_groups=Z_GROUPS, tiled=True)
    new_momentum, after = call(
        subtract,
        [array((BLOCKS * CH, CH)), array((8, CH))],
        [picked, left, momentum, inputs, grads],
        flops=2 * BLOCKS * CH * CH * TOK,
    )
    (message,) = call(
        combine,
        [array((BLOCKS * CH + BLOCKS, CH), I16)],
        [table, along_z, after],
        limit=8,
    )
    along_y = lax.all_gather(message, "rep", axis_index_groups=Y_GROUPS)
    (update,) = call(
        finish,
        [array((BLOCKS * CH, CH))],
        [along_y],
        scratch=[pltpu.VMEM((BLOCKS * CH, CH), F32), pltpu.SemaphoreType.DMA((BLOCKS // PAIR,))],
        result=pl.ANY,
    )
    return new_momentum[None], update


def solution(mesh):
    in_specs = (
        P("rep", "row", None),
        P("rep", None, "row"),
        P("rep", "row", None),
        P("rep", "row", None, None),
    )
    out_specs = (P("rep", "row", None), P("row", None))
    return jax.shard_map(body, mesh=mesh, in_specs=in_specs, out_specs=out_specs, check_vma=False)
```

```python
import jax
import jax.numpy as jnp
import numpy as np
from jax import lax
from jax.experimental import pallas as pl
from jax.experimental.pallas import tpu as pltpu
from jax.sharding import PartitionSpec as P

CH = 128
K = 8
BLOCKS = 8
PICKS = BLOCKS * K
ROWS = 8
PAIR = 2
TOK = 1024
NZ, NY = 16, 4
MOMENTUM_DECAY = 0.999
AHEAD = 10**10
BITS = 15
TOP = 32767.0
SHIFT = 2**16
WORDS = PICKS // 2
HIGHEST = lax.Precision.HIGHEST
F32, BF16, I32, I16 = jnp.float32, jnp.bfloat16, jnp.int32, jnp.int16

Z_GROUPS = [[z * NY + y for z in range(NZ)] for y in range(NY)]
Y_GROUPS = [[z * NY + y for y in range(NY)] for z in range(NZ)]


def basis_rows():
    frequency = np.arange(CH, dtype=np.float64)[:, None]
    sample = np.arange(CH, dtype=np.float64)[None, :]
    scale = np.where(frequency == 0.0, np.sqrt(1.0 / CH), np.sqrt(2.0 / CH))
    basis = scale * np.cos(np.pi * (2.0 * sample + 1.0) * frequency / (2.0 * CH))
    return np.concatenate([basis, np.zeros((8, CH))]).astype(np.float32)


def dot(a, b, dims, precision=None):
    return lax.dot_general(a, b, (dims, ((), ())), precision=precision, preferred_element_type=F32)


def halves(a):
    high = a.astype(BF16)
    return high, (a - high.astype(F32)).astype(BF16)


def block(b):
    return slice(b * CH, (b + 1) * CH)


def picks(b):
    return slice(b * K, (b + 1) * K)


def exponent(values, axis):
    most = jnp.max(jnp.abs(values), axis=axis, keepdims=True)
    return jnp.ceil(jnp.log2(jnp.maximum(most, 1e-30)) + 0.01)


def encode(values, power):
    scaled = jnp.round(values * jnp.exp2(BITS - power))
    return jnp.clip(scaled, -TOP, TOP).astype(I32)


def spread(out_grads, copies):
    for r in range(ROWS):
        copies[r, :, :] = out_grads[...]


def project(chosen, basis, momentum, inputs, grads, message, picked, left, coded, sems):
    wide = jnp.concatenate([chosen[...], jnp.zeros((BLOCKS, CH - K), I32)], axis=1)
    notes = jnp.sum(pltpu.roll(wide, 0, 1, stride=K, stride_axis=0), axis=0, keepdims=True)
    numbers = jnp.where(lax.broadcasted_iota(I32, (1, CH), 1) < PICKS, notes, CH)
    hot = jnp.where(numbers == lax.broadcasted_iota(I32, (CH, CH), 0), 1.0, 0.0).astype(BF16)
    basis_high, basis_low = halves(basis[:CH, :])
    own_high = dot(hot, basis_high, ((0,), (0,)))[:PICKS].astype(BF16)
    own_low = dot(hot, basis_low, ((0,), (0,)))[:PICKS].astype(BF16)
    picked[...] = own_high.astype(F32) + own_low.astype(F32)
    highs, lows, bases = [], [], []
    for b in range(0, BLOCKS, 2):
        pair = slice(b * CH, (b + 2) * CH)
        first = jnp.concatenate([own_high[picks(b)], own_low[picks(b)]], axis=0)
        second = jnp.concatenate([own_high[picks(b + 1)], own_low[picks(b + 1)]], axis=0)
        none = jnp.zeros_like(first)
        both = jnp.concatenate([jnp.concatenate([first, none], axis=1), jnp.concatenate([none, second], axis=1)], axis=0)
        product = dot(both, inputs[:, pair], ((1,), (1,)))
        moment_high, moment_low = halves(MOMENTUM_DECAY * momentum[pair, :])
        known = dot(both, moment_high, ((1,), (0,)))
        rest = dot(both, moment_low, ((1,), (0,)))
        for top in (0, 2 * K):
            high, low = halves(product[top : top + K] + product[top + K : top + 2 * K])
            highs.append(high)
            lows.append(low)
            bases.append(known[top : top + K] + known[top + K : top + 2 * K] + rest[top : top + K])
    product = dot(jnp.concatenate(highs + lows, axis=0), grads[...], ((1,), (0,)))
    own = jnp.concatenate(bases, axis=0) + product[:PICKS] + product[PICKS:]
    left[...] = own
    power = exponent(own, 1)
    codes = encode(own, power)
    words = [codes[picks(b), :] + codes[picks(b + 1), :] * SHIFT for b in range(0, BLOCKS, 2)]
    place = lax.broadcasted_iota(I32, (PICKS, CH), 1) == lax.broadcasted_iota(I32, (PICKS, CH), 0) + PICKS
    notes = notes + jnp.sum(jnp.where(place, power, 0.0), axis=0, keepdims=True).astype(I32)
    for i, word in enumerate(words):
        coded[picks(i), 0, :] = word
    coded[WORDS:, 0, :] = notes
    stores = [pltpu.make_async_copy(coded, message.at[z], sems.at[z]) for z in range(NZ)]
    for store in stores:
        store.start()
    for store in stores:
        store.wait()


def subtract(picked, left, momentum, inputs, grads, new_momentum, done):
    grad = dot(inputs[...], grads[...], ((0,), (0,)))
    for b in range(BLOCKS):
        sent = dot(picked[picks(b), :], left[picks(b), :], ((0,), (0,)), HIGHEST)
        new_momentum[block(b), :] = MOMENTUM_DECAY * momentum[block(b), :] + grad[block(b), :] - sent
    done[...] = picked[:8, :]


def combine(basis, received, after, message):
    del after
    notes = jnp.concatenate([received[:, WORDS, 0, :].astype(F32)] * K, axis=0).T
    own_slot = lax.broadcasted_iota(I32, (K, CH), 1) // NZ == lax.broadcasted_iota(I32, (K, CH), 0)
    notes = [jnp.sum(jnp.where(own_slot, notes[picks(i), :], 0.0), axis=0, keepdims=True) for i in range(2 * BLOCKS)]
    scales = jnp.exp2(jnp.concatenate(notes[BLOCKS:], axis=0) - BITS)
    rows = lax.broadcasted_iota(I32, (CH, NZ * K), 0).astype(F32)
    high, low = halves(basis[:CH, :].T)
    back = jnp.concatenate([high, low], axis=0)
    codes = []
    for i in range(0, WORDS, K):
        words = jnp.concatenate([received[:, i + q, 0, :] for q in range(K)], axis=0)
        even = lax.shift_right_arithmetic(lax.shift_left(words, 16), 16)
        codes += [even, lax.shift_right_arithmetic(words - even, 16)]
    powers = []
    for b in range(0, BLOCKS, 2):
        pair = []
        for i in (b, b + 1):
            hot = jnp.where(notes[i] == rows, scales[i : i + 1, :], 0.0).astype(BF16)
            sums = dot(hot, jnp.concatenate(halves(codes[i].astype(F32)), axis=1), ((1,), (0,)))
            pair.append(sums[:, :CH] + sums[:, CH:])
        own_high, own_low = halves(jnp.concatenate(pair, axis=1))
        product = dot(back, own_high, ((1,), (0,)))
        own = product[:CH] + product[CH:] + dot(high, own_low, ((1,), (0,)))
        power = exponent(own, 0)
        coded = encode(own, power).astype(I16)
        for i in (0, 1):
            powers.append(power[:, i * CH : (i + 1) * CH])
            message[block(b + i), :] = coded[:, i * CH : (i + 1) * CH]
    message[BLOCKS * CH :, :] = jnp.concatenate(powers, axis=0).astype(I32).astype(I16)


def finish(received, update, total, sems):
    scales = [jnp.exp2(received[y, BLOCKS * CH :, :].astype(I32).astype(F32) - BITS) for y in range(NY)]
    stores = []
    for b in range(BLOCKS):
        parts = [received[y, block(b), :].astype(I32).astype(F32) * scales[y][b : b + 1, :] for y in range(NY)]
        total[block(b), :] = parts[0] + parts[1] + (parts[2] + parts[3])
        if b % PAIR == PAIR - 1:
            done = slice((b + 1 - PAIR) * CH, (b + 1) * CH)
            stores.append(pltpu.make_async_copy(total.at[done, :], update.at[done, :], sems.at[b // PAIR]))
            stores[-1].start()
    for store in stores:
        store.wait()


def call(kernel, out, operands, spaces=None, flops=0, limit=4, scratch=(), results=None):
    spaces = spaces or [pltpu.VMEM] * len(operands)
    results = results or [pltpu.VMEM] * len(out)
    moved = sum(a.size * a.dtype.itemsize for a in operands) + sum(o.size * o.dtype.itemsize for o in out)
    return pl.pallas_call(
        kernel,
        name=kernel.__name__,
        out_shape=tuple(out),
        in_specs=[pl.BlockSpec(memory_space=s) for s in spaces],
        out_specs=tuple(pl.BlockSpec(memory_space=s) for s in results),
        scratch_shapes=list(scratch),
        compiler_params=pltpu.CompilerParams(vmem_limit_bytes=int(limit * 2**20)),
        cost_estimate=pl.CostEstimate(flops=flops, bytes_accessed=moved, transcendentals=0),
    )(*operands)


def array(shape, dtype=F32):
    return jax.ShapeDtypeStruct(shape, dtype)


def body(momentum, inputs, out_grads, chosen):
    momentum, inputs = momentum[0], inputs[0]
    table = jnp.asarray(basis_rows())
    (copies,) = call(spread, [array((ROWS,) + out_grads.shape[1:], BF16)], [out_grads[0]], flops=AHEAD)
    grads = lax.all_to_all(copies, "row", 0, 0, tiled=True).reshape(TOK, CH)
    message, picked, left = call(
        project,
        [array((NZ, WORDS + 1, 1, CH), I32), array((PICKS, CH)), array((PICKS, CH))],
        [chosen.reshape(BLOCKS, K), table, momentum, inputs, grads],
        flops=2 * 2 * 2 * PICKS * CH * TOK,
        scratch=[pltpu.VMEM((WORDS + 1, 1, CH), I32), pltpu.SemaphoreType.DMA((NZ,))],
        results=[pl.ANY, pltpu.VMEM, pltpu.VMEM],
    )
    along_z = lax.all_to_all(message, "rep", 0, 0, axis_index_groups=Z_GROUPS, tiled=True)
    new_momentum, after = call(
        subtract,
        [array((BLOCKS * CH, CH)), array((8, CH))],
        [picked, left, momentum, inputs, grads],
        flops=2 * BLOCKS * CH * CH * TOK,
    )
    (message,) = call(
        combine,
        [array((BLOCKS * CH + BLOCKS, CH), I16)],
        [table, along_z, after],
        limit=8,
    )
    along_y = lax.all_gather(message, "rep", axis_index_groups=Y_GROUPS)
    (update,) = call(
        finish,
        [array((BLOCKS * CH, CH))],
        [along_y],
        scratch=[pltpu.VMEM((BLOCKS * CH, CH), F32), pltpu.SemaphoreType.DMA((BLOCKS // PAIR,))],
        results=[pl.ANY],
    )
    return new_momentum[None], update


def solution(mesh):
    in_specs = (
        P("rep", "row", None),
        P("rep", None, "row"),
        P("rep", "row", None),
        P("rep", "row", None, None),
    )
    out_specs = (P("rep", "row", None), P("row", None))
    return jax.shard_map(body, mesh=mesh, in_specs=in_specs, out_specs=out_specs, check_vma=False)
```

```python
import jax
import jax.numpy as jnp
import numpy as np
from jax import lax
from jax.experimental import pallas as pl
from jax.experimental.pallas import tpu as pltpu
from jax.sharding import PartitionSpec as P

CH = 128
K = 8
BLOCKS = 8
PICKS = BLOCKS * K
ROWS = 8
PAIR = 2
TOK = 1024
NZ, NY = 16, 4
MOMENTUM_DECAY = 0.999
AHEAD = 10**10
BITS = 15
TOP = 32767.0
SHIFT = 2**16
WORDS = PICKS // 2
HIGHEST = lax.Precision.HIGHEST
F32, BF16, I32, I16 = jnp.float32, jnp.bfloat16, jnp.int32, jnp.int16

Z_GROUPS = [[z * NY + y for z in range(NZ)] for y in range(NY)]
Y_GROUPS = [[z * NY + y for y in range(NY)] for z in range(NZ)]


def basis_rows():
    frequency = np.arange(CH, dtype=np.float64)[:, None]
    sample = np.arange(CH, dtype=np.float64)[None, :]
    scale = np.where(frequency == 0.0, np.sqrt(1.0 / CH), np.sqrt(2.0 / CH))
    basis = scale * np.cos(np.pi * (2.0 * sample + 1.0) * frequency / (2.0 * CH))
    return np.concatenate([basis, np.zeros((8, CH))]).astype(np.float32)


def dot(a, b, dims, precision=None):
    return lax.dot_general(a, b, (dims, ((), ())), precision=precision, preferred_element_type=F32)


def halves(a):
    high = a.astype(BF16)
    return high, (a - high.astype(F32)).astype(BF16)


def block(b):
    return slice(b * CH, (b + 1) * CH)


def picks(b):
    return slice(b * K, (b + 1) * K)


def exponent(values, axis):
    most = jnp.max(jnp.abs(values), axis=axis, keepdims=True)
    return jnp.ceil(jnp.log2(jnp.maximum(most, 1e-30)) + 0.01)


def encode(values, power):
    scaled = jnp.round(values * jnp.exp2(BITS - power))
    return jnp.clip(scaled, -TOP, TOP).astype(I32)


def spread(out_grads, copies):
    for r in range(ROWS):
        copies[r, :, :] = out_grads[...]


def project(chosen, basis, momentum, inputs, grads, message, picked, left):
    wide = jnp.concatenate([chosen[...], jnp.zeros((BLOCKS, CH - K), I32)], axis=1)
    notes = jnp.sum(pltpu.roll(wide, 0, 1, stride=K, stride_axis=0), axis=0, keepdims=True)
    numbers = jnp.where(lax.broadcasted_iota(I32, (1, CH), 1) < PICKS, notes, CH)
    hot = jnp.where(numbers == lax.broadcasted_iota(I32, (CH, CH), 0), 1.0, 0.0).astype(BF16)
    basis_high, basis_low = halves(basis[:CH, :])
    own_high = dot(hot, basis_high, ((0,), (0,)))[:PICKS].astype(BF16)
    own_low = dot(hot, basis_low, ((0,), (0,)))[:PICKS].astype(BF16)
    picked[...] = own_high.astype(F32) + own_low.astype(F32)
    highs, lows, bases = [], [], []
    for b in range(0, BLOCKS, 2):
        pair = slice(b * CH, (b + 2) * CH)
        first = jnp.concatenate([own_high[picks(b)], own_low[picks(b)]], axis=0)
        second = jnp.concatenate([own_high[picks(b + 1)], own_low[picks(b + 1)]], axis=0)
        none = jnp.zeros_like(first)
        both = jnp.concatenate([jnp.concatenate([first, none], axis=1), jnp.concatenate([none, second], axis=1)], axis=0)
        product = dot(both, inputs[:, pair], ((1,), (1,)))
        moment_high, moment_low = halves(MOMENTUM_DECAY * momentum[pair, :])
        known = dot(both, moment_high, ((1,), (0,)))
        rest = dot(both, moment_low, ((1,), (0,)))
        for top in (0, 2 * K):
            high, low = halves(product[top : top + K] + product[top + K : top + 2 * K])
            highs.append(high)
            lows.append(low)
            bases.append(known[top : top + K] + known[top + K : top + 2 * K] + rest[top : top + K])
    product = dot(jnp.concatenate(highs + lows, axis=0), grads[...], ((1,), (0,)))
    own = jnp.concatenate(bases, axis=0) + product[:PICKS] + product[PICKS:]
    left[...] = own
    power = exponent(own, 1)
    codes = encode(own, power)
    words = [codes[picks(b), :] + codes[picks(b + 1), :] * SHIFT for b in range(0, BLOCKS, 2)]
    place = lax.broadcasted_iota(I32, (PICKS, CH), 1) == lax.broadcasted_iota(I32, (PICKS, CH), 0) + PICKS
    notes = notes + jnp.sum(jnp.where(place, power, 0.0), axis=0, keepdims=True).astype(I32)
    for z in range(NZ):
        for i, word in enumerate(words):
            message[z, picks(i), 0, :] = word
        message[z, WORDS:, 0, :] = notes


def combine(basis, received, picked, left, momentum, inputs, grads, message, new_momentum, moment, sems):
    grad = dot(grads[...], inputs[...], ((0,), (0,)))
    stores = []
    for b in range(BLOCKS):
        own_high, own_low = halves(picked[picks(b), :])
        left_high, left_low = halves(left[picks(b), :])
        own = jnp.concatenate([own_high, own_low, own_high], axis=0)
        sent = dot(own, jnp.concatenate([left_high, left_high, left_low], axis=0), ((0,), (0,)))
        moment[block(b), :] = MOMENTUM_DECAY * momentum[block(b), :] + grad[:, block(b)].T - sent
        if b % PAIR == PAIR - 1:
            done = slice((b + 1 - PAIR) * CH, (b + 1) * CH)
            stores.append(pltpu.make_async_copy(moment.at[done, :], new_momentum.at[done, :], sems.at[b // PAIR]))
            stores[-1].start()
    notes = jnp.concatenate([received[:, WORDS, 0, :].astype(F32)] * K, axis=0).T
    own_slot = lax.broadcasted_iota(I32, (K, CH), 1) // NZ == lax.broadcasted_iota(I32, (K, CH), 0)
    notes = [jnp.sum(jnp.where(own_slot, notes[picks(i), :], 0.0), axis=0, keepdims=True) for i in range(2 * BLOCKS)]
    scales = jnp.exp2(jnp.concatenate(notes[BLOCKS:], axis=0) - BITS)
    rows = lax.broadcasted_iota(I32, (CH, NZ * K), 0).astype(F32)
    high, low = halves(basis[:CH, :].T)
    back = jnp.concatenate([high, low], axis=0)
    codes = []
    for i in range(0, WORDS, K):
        words = jnp.concatenate([received[:, i + q, 0, :] for q in range(K)], axis=0)
        even = lax.shift_right_arithmetic(lax.shift_left(words, 16), 16)
        codes += [even, lax.shift_right_arithmetic(words - even, 16)]
    powers = []
    for b in range(0, BLOCKS, 2):
        pair = []
        for i in (b, b + 1):
            hot = jnp.where(notes[i] == rows, scales[i : i + 1, :], 0.0).astype(BF16)
            sums = dot(hot, jnp.concatenate(halves(codes[i].astype(F32)), axis=1), ((1,), (0,)))
            pair.append(sums[:, :CH] + sums[:, CH:])
        own_high, own_low = halves(jnp.concatenate(pair, axis=1))
        product = dot(back, own_high, ((1,), (0,)))
        own = product[:CH] + product[CH:] + dot(high, own_low, ((1,), (0,)))
        power = exponent(own, 0)
        coded = encode(own, power).astype(I16)
        for i in (0, 1):
            powers.append(power[:, i * CH : (i + 1) * CH])
            message[block(b + i), :] = coded[:, i * CH : (i + 1) * CH]
    message[BLOCKS * CH :, :] = jnp.concatenate(powers, axis=0).astype(I32).astype(I16)
    for store in stores:
        store.wait()


def finish(received, update, total, sems):
    scales = [jnp.exp2(received[y, BLOCKS * CH :, :].astype(I32).astype(F32) - BITS) for y in range(NY)]
    stores = []
    for b in range(BLOCKS):
        parts = [received[y, block(b), :].astype(I32).astype(F32) * scales[y][b : b + 1, :] for y in range(NY)]
        total[block(b), :] = parts[0] + parts[1] + (parts[2] + parts[3])
        if b % PAIR == PAIR - 1:
            done = slice((b + 1 - PAIR) * CH, (b + 1) * CH)
            stores.append(pltpu.make_async_copy(total.at[done, :], update.at[done, :], sems.at[b // PAIR]))
            stores[-1].start()
    for store in stores:
        store.wait()


def call(kernel, out, operands, spaces=None, flops=0, limit=4, scratch=(), results=None):
    spaces = spaces or [pltpu.VMEM] * len(operands)
    results = results or [pltpu.VMEM] * len(out)
    moved = sum(a.size * a.dtype.itemsize for a in operands) + sum(o.size * o.dtype.itemsize for o in out)
    return pl.pallas_call(
        kernel,
        name=kernel.__name__,
        out_shape=tuple(out),
        in_specs=[pl.BlockSpec(memory_space=s) for s in spaces],
        out_specs=tuple(pl.BlockSpec(memory_space=s) for s in results),
        scratch_shapes=list(scratch),
        compiler_params=pltpu.CompilerParams(vmem_limit_bytes=int(limit * 2**20)),
        cost_estimate=pl.CostEstimate(flops=flops, bytes_accessed=moved, transcendentals=0),
    )(*operands)


def array(shape, dtype=F32):
    return jax.ShapeDtypeStruct(shape, dtype)


def body(momentum, inputs, out_grads, chosen):
    momentum, inputs = momentum[0], inputs[0]
    table = jnp.asarray(basis_rows())
    (copies,) = call(spread, [array((ROWS,) + out_grads.shape[1:], BF16)], [out_grads[0]], flops=AHEAD)
    grads = lax.all_to_all(copies, "row", 0, 0, tiled=True).reshape(TOK, CH)
    message, picked, left = call(
        project,
        [array((NZ, WORDS + 1, 1, CH), I32), array((PICKS, CH)), array((PICKS, CH))],
        [chosen.reshape(BLOCKS, K), table, momentum, inputs, grads],
        flops=2 * 2 * 2 * PICKS * CH * TOK,
    )
    along_z = lax.all_to_all(message, "rep", 0, 0, axis_index_groups=Z_GROUPS, tiled=True)
    message, new_momentum = call(
        combine,
        [array((BLOCKS * CH + BLOCKS, CH), I16), array((BLOCKS * CH, CH))],
        [table, along_z, picked, left, momentum, inputs, grads],
        limit=8,
        flops=2 * BLOCKS * CH * CH * TOK,
        scratch=[pltpu.VMEM((BLOCKS * CH, CH), F32), pltpu.SemaphoreType.DMA((BLOCKS // PAIR,))],
        results=[pltpu.VMEM, pl.ANY],
    )
    along_y = lax.all_gather(message, "rep", axis_index_groups=Y_GROUPS)
    (update,) = call(
        finish,
        [array((BLOCKS * CH, CH))],
        [along_y],
        scratch=[pltpu.VMEM((BLOCKS * CH, CH), F32), pltpu.SemaphoreType.DMA((BLOCKS // PAIR,))],
        results=[pl.ANY],
    )
    return new_momentum[None], update


def solution(mesh):
    in_specs = (
        P("rep", "row", None),
        P("rep", None, "row"),
        P("rep", "row", None),
        P("rep", "row", None, None),
    )
    out_specs = (P("rep", "row", None), P("row", None))
    return jax.shard_map(body, mesh=mesh, in_specs=in_specs, out_specs=out_specs, check_vma=False)
```

```python
import jax
import jax.numpy as jnp
import numpy as np
from jax import lax
from jax.experimental import pallas as pl
from jax.experimental.pallas import tpu as pltpu
from jax.sharding import PartitionSpec as P

CH = 128
K = 8
BLOCKS = 8
PICKS = BLOCKS * K
ROWS = 8
PAIR = 2
TOK = 1024
NZ, NY = 16, 4
EARLY = 32
MOMENTUM_DECAY = 0.999
AHEAD = 10**10
BITS = 15
TOP = 32767.0
SHIFT = 2**16
WORDS = PICKS // 2
HIGHEST = lax.Precision.HIGHEST
F32, BF16, I32, I16 = jnp.float32, jnp.bfloat16, jnp.int32, jnp.int16

Z_GROUPS = [[z * NY + y for z in range(NZ)] for y in range(NY)]
Y_GROUPS = [[z * NY + y for y in range(NY)] for z in range(NZ)]


def basis_rows():
    frequency = np.arange(CH, dtype=np.float64)[:, None]
    sample = np.arange(CH, dtype=np.float64)[None, :]
    scale = np.where(frequency == 0.0, np.sqrt(1.0 / CH), np.sqrt(2.0 / CH))
    basis = scale * np.cos(np.pi * (2.0 * sample + 1.0) * frequency / (2.0 * CH))
    return np.concatenate([basis, np.zeros((8, CH))]).astype(np.float32)


def dot(a, b, dims, precision=None):
    return lax.dot_general(a, b, (dims, ((), ())), precision=precision, preferred_element_type=F32)


def halves(a):
    high = a.astype(BF16)
    return high, (a - high.astype(F32)).astype(BF16)


def block(b):
    return slice(b * CH, (b + 1) * CH)


def picks(b):
    return slice(b * K, (b + 1) * K)


def exponent(values, axis):
    most = jnp.max(jnp.abs(values), axis=axis, keepdims=True)
    return jnp.ceil(jnp.log2(jnp.maximum(most, 1e-30)) + 0.01)


def encode(values, power):
    scaled = jnp.round(values * jnp.exp2(BITS - power))
    return jnp.clip(scaled, -TOP, TOP).astype(I32)


def spread(out_grads, copies):
    for r in range(ROWS):
        copies[r, :, :] = out_grads[...]


def subtract(picked, left, momentum, inputs, grads, new_momentum, moment, sems):
    grad = dot(grads[...], inputs[...], ((0,), (0,)))
    stores = []
    for b in range(BLOCKS):
        own_high, own_low = halves(picked[picks(b), :])
        left_high, left_low = halves(left[picks(b), :])
        own = jnp.concatenate([own_high, own_low, own_high], axis=0)
        sent = dot(own, jnp.concatenate([left_high, left_high, left_low], axis=0), ((0,), (0,)))
        moment[block(b), :] = MOMENTUM_DECAY * momentum[block(b), :] + grad[:, block(b)].T - sent
        if b % PAIR == PAIR - 1:
            done = slice((b + 1 - PAIR) * CH, (b + 1) * CH)
            stores.append(pltpu.make_async_copy(moment.at[done, :], new_momentum.at[done, :], sems.at[b // PAIR]))
            stores[-1].start()
    for store in stores:
        store.wait()


def project(chosen, basis, momentum, inputs, grads, message, picked, left, new_momentum, moment, sems):
    wide = jnp.concatenate([chosen[...], jnp.zeros((BLOCKS, CH - K), I32)], axis=1)
    notes = jnp.sum(pltpu.roll(wide, 0, 1, stride=K, stride_axis=0), axis=0, keepdims=True)
    numbers = jnp.where(lax.broadcasted_iota(I32, (1, CH), 1) < PICKS, notes, CH)
    hot = jnp.where(numbers == lax.broadcasted_iota(I32, (CH, CH), 0), 1.0, 0.0).astype(BF16)
    basis_high, basis_low = halves(basis[:CH, :])
    own_high = dot(hot, basis_high, ((0,), (0,)))[:PICKS].astype(BF16)
    own_low = dot(hot, basis_low, ((0,), (0,)))[:PICKS].astype(BF16)
    picked[...] = own_high.astype(F32) + own_low.astype(F32)
    highs, lows, bases = [], [], []
    for b in range(0, BLOCKS, 2):
        pair = slice(b * CH, (b + 2) * CH)
        first = jnp.concatenate([own_high[picks(b)], own_low[picks(b)]], axis=0)
        second = jnp.concatenate([own_high[picks(b + 1)], own_low[picks(b + 1)]], axis=0)
        none = jnp.zeros_like(first)
        both = jnp.concatenate([jnp.concatenate([first, none], axis=1), jnp.concatenate([none, second], axis=1)], axis=0)
        product = dot(both, inputs[:, pair], ((1,), (1,)))
        moment_high, moment_low = halves(MOMENTUM_DECAY * momentum[pair, :])
        known = dot(both, moment_high, ((1,), (0,)))
        rest = dot(both, moment_low, ((1,), (0,)))
        for top in (0, 2 * K):
            high, low = halves(product[top : top + K] + product[top + K : top + 2 * K])
            highs.append(high)
            lows.append(low)
            bases.append(known[top : top + K] + known[top + K : top + 2 * K] + rest[top : top + K])
    product = dot(jnp.concatenate(highs + lows, axis=0), grads[...], ((1,), (0,)))
    own = jnp.concatenate(bases, axis=0) + product[:PICKS] + product[PICKS:]
    left[...] = own
    power = exponent(own, 1)
    codes = encode(own, power)
    words = [codes[picks(b), :] + codes[picks(b + 1), :] * SHIFT for b in range(0, BLOCKS, 2)]
    place = lax.broadcasted_iota(I32, (PICKS, CH), 1) == lax.broadcasted_iota(I32, (PICKS, CH), 0) + PICKS
    notes = notes + jnp.sum(jnp.where(place, power, 0.0), axis=0, keepdims=True).astype(I32)
    for z in range(NZ):
        for i, word in enumerate(words):
            message[z, picks(i), 0, :] = word
        message[z, WORDS:, 0, :] = notes

    @pl.when(lax.axis_index("rep") < EARLY)
    def _():
        subtract(picked, left, momentum, inputs, grads, new_momentum, moment, sems)


def combine(basis, received, picked, left, momentum, inputs, grads, begun, message, new_momentum, moment, sems):
    del begun
    @pl.when(lax.axis_index("rep") >= EARLY)
    def _():
        subtract(picked, left, momentum, inputs, grads, new_momentum, moment, sems)

    notes = jnp.concatenate([received[:, WORDS, 0, :].astype(F32)] * K, axis=0).T
    own_slot = lax.broadcasted_iota(I32, (K, CH), 1) // NZ == lax.broadcasted_iota(I32, (K, CH), 0)
    notes = [jnp.sum(jnp.where(own_slot, notes[picks(i), :], 0.0), axis=0, keepdims=True) for i in range(2 * BLOCKS)]
    scales = jnp.exp2(jnp.concatenate(notes[BLOCKS:], axis=0) - BITS)
    rows = lax.broadcasted_iota(I32, (CH, NZ * K), 0).astype(F32)
    high, low = halves(basis[:CH, :].T)
    back = jnp.concatenate([high, low], axis=0)
    codes = []
    for i in range(0, WORDS, K):
        words = jnp.concatenate([received[:, i + q, 0, :] for q in range(K)], axis=0)
        even = lax.shift_right_arithmetic(lax.shift_left(words, 16), 16)
        codes += [even, lax.shift_right_arithmetic(words - even, 16)]
    powers = []
    for b in range(0, BLOCKS, 2):
        pair = []
        for i in (b, b + 1):
            hot = jnp.where(notes[i] == rows, scales[i : i + 1, :], 0.0).astype(BF16)
            sums = dot(hot, jnp.concatenate(halves(codes[i].astype(F32)), axis=1), ((1,), (0,)))
            pair.append(sums[:, :CH] + sums[:, CH:])
        own_high, own_low = halves(jnp.concatenate(pair, axis=1))
        product = dot(back, own_high, ((1,), (0,)))
        own = product[:CH] + product[CH:] + dot(high, own_low, ((1,), (0,)))
        power = exponent(own, 0)
        coded = encode(own, power).astype(I16)
        for i in (0, 1):
            powers.append(power[:, i * CH : (i + 1) * CH])
            message[block(b + i), :] = coded[:, i * CH : (i + 1) * CH]
    message[BLOCKS * CH :, :] = jnp.concatenate(powers, axis=0).astype(I32).astype(I16)


def finish(received, update, total, sems):
    scales = [jnp.exp2(received[y, BLOCKS * CH :, :].astype(I32).astype(F32) - BITS) for y in range(NY)]
    stores = []
    for b in range(BLOCKS):
        parts = [received[y, block(b), :].astype(I32).astype(F32) * scales[y][b : b + 1, :] for y in range(NY)]
        total[block(b), :] = parts[0] + parts[1] + (parts[2] + parts[3])
        if b % PAIR == PAIR - 1:
            done = slice((b + 1 - PAIR) * CH, (b + 1) * CH)
            stores.append(pltpu.make_async_copy(total.at[done, :], update.at[done, :], sems.at[b // PAIR]))
            stores[-1].start()
    for store in stores:
        store.wait()


def call(kernel, out, operands, spaces=None, flops=0, limit=4, scratch=(), results=None, aliases=None):
    spaces = spaces or [pltpu.VMEM] * len(operands)
    results = results or [pltpu.VMEM] * len(out)
    moved = sum(a.size * a.dtype.itemsize for a in operands) + sum(o.size * o.dtype.itemsize for o in out)
    return pl.pallas_call(
        kernel,
        name=kernel.__name__,
        out_shape=tuple(out),
        in_specs=[pl.BlockSpec(memory_space=s) for s in spaces],
        out_specs=tuple(pl.BlockSpec(memory_space=s) for s in results),
        scratch_shapes=list(scratch),
        input_output_aliases=aliases or {},
        compiler_params=pltpu.CompilerParams(vmem_limit_bytes=int(limit * 2**20)),
        cost_estimate=pl.CostEstimate(flops=flops, bytes_accessed=moved, transcendentals=0),
    )(*operands)


def array(shape, dtype=F32):
    return jax.ShapeDtypeStruct(shape, dtype)


def body(momentum, inputs, out_grads, chosen):
    momentum, inputs = momentum[0], inputs[0]
    table = jnp.asarray(basis_rows())
    (copies,) = call(spread, [array((ROWS,) + out_grads.shape[1:], BF16)], [out_grads[0]], flops=AHEAD)
    grads = lax.all_to_all(copies, "row", 0, 0, tiled=True).reshape(TOK, CH)
    message, picked, left, new_momentum = call(
        project,
        [array((NZ, WORDS + 1, 1, CH), I32), array((PICKS, CH)), array((PICKS, CH)), array((BLOCKS * CH, CH))],
        [chosen.reshape(BLOCKS, K), table, momentum, inputs, grads],
        flops=2 * 2 * 2 * PICKS * CH * TOK,
        limit=8,
        scratch=[pltpu.VMEM((BLOCKS * CH, CH), F32), pltpu.SemaphoreType.DMA((BLOCKS // PAIR,))],
        results=[pltpu.VMEM, pltpu.VMEM, pltpu.VMEM, pl.ANY],
    )
    along_z = lax.all_to_all(message, "rep", 0, 0, axis_index_groups=Z_GROUPS, tiled=True)
    message, new_momentum = call(
        combine,
        [array((BLOCKS * CH + BLOCKS, CH), I16), array((BLOCKS * CH, CH))],
        [table, along_z, picked, left, momentum, inputs, grads, new_momentum],
        spaces=[pltpu.VMEM] * 7 + [pl.ANY],
        aliases={7: 1},
        limit=8,
        flops=2 * BLOCKS * CH * CH * TOK,
        scratch=[pltpu.VMEM((BLOCKS * CH, CH), F32), pltpu.SemaphoreType.DMA((BLOCKS // PAIR,))],
        results=[pltpu.VMEM, pl.ANY],
    )
    along_y = lax.all_gather(message, "rep", axis_index_groups=Y_GROUPS)
    (update,) = call(
        finish,
        [array((BLOCKS * CH, CH))],
        [along_y],
        scratch=[pltpu.VMEM((BLOCKS * CH, CH), F32), pltpu.SemaphoreType.DMA((BLOCKS // PAIR,))],
        results=[pl.ANY],
    )
    return new_momentum[None], update


def solution(mesh):
    in_specs = (
        P("rep", "row", None),
        P("rep", None, "row"),
        P("rep", "row", None),
        P("rep", "row", None, None),
    )
    out_specs = (P("rep", "row", None), P("row", None))
    return jax.shard_map(body, mesh=mesh, in_specs=in_specs, out_specs=out_specs, check_vma=False)
```

```python
import jax
import jax.numpy as jnp
import numpy as np
from jax import lax
from jax.experimental import pallas as pl
from jax.experimental.pallas import tpu as pltpu
from jax.sharding import PartitionSpec as P

CH = 128
K = 8
BLOCKS = 8
PICKS = BLOCKS * K
ROWS = 8
PAIR = 1
TOK = 1024
NZ, NY = 16, 4
EARLY = 32
MOMENTUM_DECAY = 0.999
AHEAD = 10**10
BITS = 15
TOP = 32767.0
SHIFT = 2**16
WORDS = PICKS // 2
HIGHEST = lax.Precision.HIGHEST
F32, BF16, I32, I16 = jnp.float32, jnp.bfloat16, jnp.int32, jnp.int16

Z_GROUPS = [[z * NY + y for z in range(NZ)] for y in range(NY)]
Y_GROUPS = [[z * NY + y for y in range(NY)] for z in range(NZ)]


def basis_rows():
    frequency = np.arange(CH, dtype=np.float64)[:, None]
    sample = np.arange(CH, dtype=np.float64)[None, :]
    scale = np.where(frequency == 0.0, np.sqrt(1.0 / CH), np.sqrt(2.0 / CH))
    basis = scale * np.cos(np.pi * (2.0 * sample + 1.0) * frequency / (2.0 * CH))
    return np.concatenate([basis, np.zeros((8, CH))]).astype(np.float32)


def dot(a, b, dims, precision=None):
    return lax.dot_general(a, b, (dims, ((), ())), precision=precision, preferred_element_type=F32)


def halves(a):
    high = a.astype(BF16)
    return high, (a - high.astype(F32)).astype(BF16)


def block(b):
    return slice(b * CH, (b + 1) * CH)


def picks(b):
    return slice(b * K, (b + 1) * K)


def exponent(values, axis):
    most = jnp.max(jnp.abs(values), axis=axis, keepdims=True)
    return jnp.ceil(jnp.log2(jnp.maximum(most, 1e-30)) + 0.01)


def encode(values, power):
    scaled = jnp.round(values * jnp.exp2(BITS - power))
    return jnp.clip(scaled, -TOP, TOP).astype(I32)


def spread(out_grads, copies):
    for r in range(ROWS):
        copies[r, :, :] = out_grads[...]


def subtract(picked, left, momentum, inputs, grads, new_momentum, moment, sems):
    grad = dot(grads[...], inputs[...], ((0,), (0,)))
    stores = []
    for b in range(BLOCKS):
        own_high, own_low = halves(picked[picks(b), :])
        left_high, left_low = halves(left[picks(b), :])
        own = jnp.concatenate([own_high, own_low, own_high], axis=0)
        sent = dot(own, jnp.concatenate([left_high, left_high, left_low], axis=0), ((0,), (0,)))
        moment[block(b), :] = MOMENTUM_DECAY * momentum[block(b), :] + grad[:, block(b)].T - sent
        if b % PAIR == PAIR - 1:
            done = slice((b + 1 - PAIR) * CH, (b + 1) * CH)
            stores.append(pltpu.make_async_copy(moment.at[done, :], new_momentum.at[done, :], sems.at[b // PAIR]))
            stores[-1].start()
    for store in stores:
        store.wait()


def project(chosen, basis, momentum, inputs, grads, message, picked, left, new_momentum, moment, sems):
    wide = jnp.concatenate([chosen[...], jnp.zeros((BLOCKS, CH - K), I32)], axis=1)
    notes = jnp.sum(pltpu.roll(wide, 0, 1, stride=K, stride_axis=0), axis=0, keepdims=True)
    numbers = jnp.where(lax.broadcasted_iota(I32, (1, CH), 1) < PICKS, notes, CH)
    hot = jnp.where(numbers == lax.broadcasted_iota(I32, (CH, CH), 0), 1.0, 0.0).astype(BF16)
    basis_high, basis_low = halves(basis[:CH, :])
    own_high = dot(hot, basis_high, ((0,), (0,)))[:PICKS].astype(BF16)
    own_low = dot(hot, basis_low, ((0,), (0,)))[:PICKS].astype(BF16)
    picked[...] = own_high.astype(F32) + own_low.astype(F32)
    highs, lows, bases = [], [], []
    for b in range(0, BLOCKS, 2):
        pair = slice(b * CH, (b + 2) * CH)
        first = jnp.concatenate([own_high[picks(b)], own_low[picks(b)]], axis=0)
        second = jnp.concatenate([own_high[picks(b + 1)], own_low[picks(b + 1)]], axis=0)
        none = jnp.zeros_like(first)
        both = jnp.concatenate([jnp.concatenate([first, none], axis=1), jnp.concatenate([none, second], axis=1)], axis=0)
        product = dot(both, inputs[:, pair], ((1,), (1,)))
        moment_high, moment_low = halves(MOMENTUM_DECAY * momentum[pair, :])
        known = dot(both, moment_high, ((1,), (0,)))
        rest = dot(both, moment_low, ((1,), (0,)))
        for top in (0, 2 * K):
            high, low = halves(product[top : top + K] + product[top + K : top + 2 * K])
            highs.append(high)
            lows.append(low)
            bases.append(known[top : top + K] + known[top + K : top + 2 * K] + rest[top : top + K])
    product = dot(jnp.concatenate(highs + lows, axis=0), grads[...], ((1,), (0,)))
    own = jnp.concatenate(bases, axis=0) + product[:PICKS] + product[PICKS:]
    left[...] = own
    power = exponent(own, 1)
    codes = encode(own, power)
    words = [codes[picks(b), :] + codes[picks(b + 1), :] * SHIFT for b in range(0, BLOCKS, 2)]
    place = lax.broadcasted_iota(I32, (PICKS, CH), 1) == lax.broadcasted_iota(I32, (PICKS, CH), 0) + PICKS
    notes = notes + jnp.sum(jnp.where(place, power, 0.0), axis=0, keepdims=True).astype(I32)
    for z in range(NZ):
        for i, word in enumerate(words):
            message[z, picks(i), 0, :] = word
        message[z, WORDS:, 0, :] = notes

    @pl.when(lax.axis_index("rep") < EARLY)
    def _():
        subtract(picked, left, momentum, inputs, grads, new_momentum, moment, sems)


def combine(basis, received, picked, left, momentum, inputs, grads, begun, message, new_momentum, moment, sems):
    del begun
    @pl.when(lax.axis_index("rep") >= EARLY)
    def _():
        subtract(picked, left, momentum, inputs, grads, new_momentum, moment, sems)

    notes = jnp.concatenate([received[:, WORDS, 0, :].astype(F32)] * K, axis=0).T
    own_slot = lax.broadcasted_iota(I32, (K, CH), 1) // NZ == lax.broadcasted_iota(I32, (K, CH), 0)
    notes = [jnp.sum(jnp.where(own_slot, notes[picks(i), :], 0.0), axis=0, keepdims=True) for i in range(2 * BLOCKS)]
    scales = jnp.exp2(jnp.concatenate(notes[BLOCKS:], axis=0) - BITS)
    rows = lax.broadcasted_iota(I32, (CH, NZ * K), 0).astype(F32)
    high, low = halves(basis[:CH, :].T)
    back = jnp.concatenate([high, low], axis=0)
    codes = []
    for i in range(0, WORDS, K):
        words = jnp.concatenate([received[:, i + q, 0, :] for q in range(K)], axis=0)
        even = lax.shift_right_arithmetic(lax.shift_left(words, 16), 16)
        codes += [even, lax.shift_right_arithmetic(words - even, 16)]
    powers = []
    for b in range(0, BLOCKS, 2):
        pair = []
        for i in (b, b + 1):
            hot = jnp.where(notes[i] == rows, scales[i : i + 1, :], 0.0).astype(BF16)
            sums = dot(hot, jnp.concatenate(halves(codes[i].astype(F32)), axis=1), ((1,), (0,)))
            pair.append(sums[:, :CH] + sums[:, CH:])
        own_high, own_low = halves(jnp.concatenate(pair, axis=1))
        product = dot(back, own_high, ((1,), (0,)))
        own = product[:CH] + product[CH:] + dot(high, own_low, ((1,), (0,)))
        power = exponent(own, 0)
        coded = encode(own, power).astype(I16)
        for i in (0, 1):
            powers.append(power[:, i * CH : (i + 1) * CH])
            message[block(b + i), :] = coded[:, i * CH : (i + 1) * CH]
    message[BLOCKS * CH :, :] = jnp.concatenate(powers, axis=0).astype(I32).astype(I16)


def finish(received, update, total, sems):
    scales = [jnp.exp2(received[y, BLOCKS * CH :, :].astype(I32).astype(F32) - BITS) for y in range(NY)]
    stores = []
    for b in range(BLOCKS):
        parts = [received[y, block(b), :].astype(I32).astype(F32) * scales[y][b : b + 1, :] for y in range(NY)]
        total[block(b), :] = parts[0] + parts[1] + (parts[2] + parts[3])
        if b % PAIR == PAIR - 1:
            done = slice((b + 1 - PAIR) * CH, (b + 1) * CH)
            stores.append(pltpu.make_async_copy(total.at[done, :], update.at[done, :], sems.at[b // PAIR]))
            stores[-1].start()
    for store in stores:
        store.wait()


def call(kernel, out, operands, spaces=None, flops=0, limit=4, scratch=(), results=None, aliases=None):
    spaces = spaces or [pltpu.VMEM] * len(operands)
    results = results or [pltpu.VMEM] * len(out)
    moved = sum(a.size * a.dtype.itemsize for a in operands) + sum(o.size * o.dtype.itemsize for o in out)
    return pl.pallas_call(
        kernel,
        name=kernel.__name__,
        out_shape=tuple(out),
        in_specs=[pl.BlockSpec(memory_space=s) for s in spaces],
        out_specs=tuple(pl.BlockSpec(memory_space=s) for s in results),
        scratch_shapes=list(scratch),
        input_output_aliases=aliases or {},
        compiler_params=pltpu.CompilerParams(vmem_limit_bytes=int(limit * 2**20)),
        cost_estimate=pl.CostEstimate(flops=flops, bytes_accessed=moved, transcendentals=0),
    )(*operands)


def array(shape, dtype=F32):
    return jax.ShapeDtypeStruct(shape, dtype)


def body(momentum, inputs, out_grads, chosen):
    momentum, inputs = momentum[0], inputs[0]
    table = jnp.asarray(basis_rows())
    (copies,) = call(spread, [array((ROWS,) + out_grads.shape[1:], BF16)], [out_grads[0]], flops=AHEAD)
    grads = lax.all_to_all(copies, "row", 0, 0, tiled=True).reshape(TOK, CH)
    message, picked, left, new_momentum = call(
        project,
        [array((NZ, WORDS + 1, 1, CH), I32), array((PICKS, CH)), array((PICKS, CH)), array((BLOCKS * CH, CH))],
        [chosen.reshape(BLOCKS, K), table, momentum, inputs, grads],
        flops=2 * 2 * 2 * PICKS * CH * TOK,
        limit=8,
        scratch=[pltpu.VMEM((BLOCKS * CH, CH), F32), pltpu.SemaphoreType.DMA((BLOCKS // PAIR,))],
        results=[pltpu.VMEM, pltpu.VMEM, pltpu.VMEM, pl.ANY],
    )
    along_z = lax.all_to_all(message, "rep", 0, 0, axis_index_groups=Z_GROUPS, tiled=True)
    message, new_momentum = call(
        combine,
        [array((BLOCKS * CH + BLOCKS, CH), I16), array((BLOCKS * CH, CH))],
        [table, along_z, picked, left, momentum, inputs, grads, new_momentum],
        spaces=[pltpu.VMEM] * 7 + [pl.ANY],
        aliases={7: 1},
        limit=8,
        flops=2 * BLOCKS * CH * CH * TOK,
        scratch=[pltpu.VMEM((BLOCKS * CH, CH), F32), pltpu.SemaphoreType.DMA((BLOCKS // PAIR,))],
        results=[pltpu.VMEM, pl.ANY],
    )
    along_y = lax.all_gather(message, "rep", axis_index_groups=Y_GROUPS)
    (update,) = call(
        finish,
        [array((BLOCKS * CH, CH))],
        [along_y],
        scratch=[pltpu.VMEM((BLOCKS * CH, CH), F32), pltpu.SemaphoreType.DMA((BLOCKS // PAIR,))],
        results=[pl.ANY],
    )
    return new_momentum[None], update


def solution(mesh):
    in_specs = (
        P("rep", "row", None),
        P("rep", None, "row"),
        P("rep", "row", None),
        P("rep", "row", None, None),
    )
    out_specs = (P("rep", "row", None), P("row", None))
    return jax.shard_map(body, mesh=mesh, in_specs=in_specs, out_specs=out_specs, check_vma=False)
```
